32 devices in a mesh: groups: 2 (over x), branch: 16 (over z, y, core).
Axes of the slice: x: 2, y: 2, z: 4, core: 2. Of those that a mesh axis runs over, the one named last changes fastest.
Arguments:
- prompt_k: bfloat16 [32, 1024, 1024], P(('groups', 'branch')), parts along dimension 0, may hold values from -6 to 6
- prompt_v: bfloat16 [32, 1024, 1024], P(('groups', 'branch')), parts along dimension 0, may hold values from -6 to 6
- prompt_mask: int32 [32, 8], P(('groups', 'branch')), parts along dimension 0, may hold values from 0 to 1, as said below
- shared_kv: bfloat16 [64, 24, 2048], P(('groups', 'branch')), parts along dimension 0, may hold values from -6 to 6
- shared_len: int32 [64], P(('groups', 'branch')), parts along dimension 0, may hold values from 1 to 24, 400 in all
- send_pick: int32 [32, 16], P(('groups', 'branch')), parts along dimension 0, may hold values from -1 to 1, as said below
- unique_q: bfloat16 [512, 8192], P(('groups', 'branch')), parts along dimension 0, may hold values from -132 to 132
- unique_kv: bfloat16 [512, 2048], P(('groups', 'branch')), parts along dimension 0, may hold values from -6.5 to 6.5
- unique_owner: int32 [512, 1], P(('groups', 'branch')), parts along dimension 0, may hold values from 0 to 15; in each aligned block of 16 rows (0 to 15, 16 to 31, ...) at most 2 rows name the same one
Outputs:
- attended: bfloat16 [512, 8192], P(('groups', 'branch')), parts along dimension 0
The draws below stay inside these ranges and needn't reach their ends.
There are 2 independent parts, one for each index of `groups`. The reference program is written for one: setup_inputs(seed, part) draws one part's arguments, and reference() takes and returns one part's arrays. A program takes and returns all parts, laid end to end along the dimension named above; each array names one. Nothing has to cross between parts.
Inputs may be any that keep to these rules, and one draw needn't show every extreme that they name: `prompt_mask`: block 0 of every branch's prompt is visible. `send_pick`: entry [s, b] names which of owner s's 2 results branch b subscribes to, or -1 for none; every branch subscribes to exactly 12 results, at most one of each owner. `unique_owner`: among the rows of one source, no branch is named by more than 2 rows.
All inputs are finite; a program needn't handle non-finite values. No bound on the sum of `shared_len` on one device may be relied on, other than what follows from the above.
Results may differ from the reference program's by a relative error of at most 0.0027.
Values may be sent and summed in bfloat16 or wider, within the bound.
A program may use at most 128 MiB of HBM per device.

```python
import math
import jax
import jax.numpy as jnp
import numpy as np
from jax import lax

QH = 64
KVH = 8
HD = 128
GRP = 8
QW = 8192
KVW = 1024
PLEN = 1024
PB = 128
PBLK = 8
RLEN = 24
RES_DEV = 2
NRES = 32
SUBS = 12
CAP = 2
UNQ_DEV = 16
ROWS = 256
N_BRANCH = 16


def draw_prompt_k(key, part):
    values = jnp.clip(jax.random.normal(jax.random.fold_in(key, 11), (N_BRANCH, PLEN, KVW), jnp.float32), -6.0, 6.0)
    return values.astype(jnp.bfloat16)


def draw_prompt_mask(key, part):
    levels = jax.random.randint(jax.random.fold_in(key, 19), (N_BRANCH, PBLK), 0, 4)
    visible = (levels > 0).astype(jnp.int32)
    return visible.at[:, 0].set(1)


def draw_send_pick(key, part):
    subkeys = jax.random.split(jax.random.fold_in(key, 23), N_BRANCH)
    ordering = jax.vmap(lambda single: jax.random.permutation(single, N_BRANCH))(subkeys)
    position = jnp.argsort(ordering, axis=1)
    which = jax.random.randint(jax.random.fold_in(key, 29), (N_BRANCH, N_BRANCH), 0, RES_DEV)
    picked = jnp.where(position < SUBS, which, -1)
    return picked.T.astype(jnp.int32)


def draw_unique_q(key, part):
    values = 3.0 * jnp.clip(jax.random.normal(jax.random.fold_in(key, 13), (ROWS, QW), jnp.float32), -6.0, 6.0)
    return values.astype(jnp.bfloat16)


def draw_unique_kv(key, part):
    values = jnp.clip(jax.random.normal(jax.random.fold_in(key, 17), (ROWS, 2 * KVW), jnp.float32), -6.0, 6.0)
    return values.astype(jnp.bfloat16)


def block_scale(stream_key, dims, cuts, least, top_value):
    level = 1.0
    for dim, shards_of in cuts:
        steps = jax.random.uniform(jax.random.fold_in(jax.random.fold_in(stream_key, 6), dim), (shards_of,), jnp.float32, least / len(cuts), top_value / len(cuts))
        level = level * jnp.repeat(jnp.exp(steps), dims[dim] // shards_of).reshape((-1,) + (1,) * (len(dims) - 1 - dim))
    return level


def split_up(amount, total, reach, skew):
    portions = [(1 << 20) // math.isqrt(rank ** skew) + 1 for rank in range(2, amount + 1)]
    surplus, counts = total - reach - (amount - 1), [1] * (amount - 1)
    while surplus > 0:
        candidates = [i for i in range(amount - 1) if counts[i] < reach]
        mass, budget = sum([portions[i] for i in candidates]), surplus
        for i in candidates:
            more = min(reach - counts[i], max(1, budget * portions[i] // mass), surplus)
            counts[i] = counts[i] + more
            surplus = surplus - more
    return np.array([reach] + counts)


def ragged_sizes(stream_key, number_of, total, most, slope):
    if number_of == 2:
        one = jax.random.randint(stream_key, (), max(1, total - most), min(most, total - 1) + 1)
        return jnp.stack([one, total - one])
    sizes = jnp.asarray(split_up(number_of, total, most, slope), jnp.int32)
    pairs = (number_of - 1) // 2
    source_of, sink = sizes[1:1 + 2 * pairs:2], sizes[2:2 + 2 * pairs:2]
    margin = jnp.minimum(source_of - 1, most - sink)
    shifted = jax.random.randint(jax.random.fold_in(stream_key, 1), (pairs,), 0, 1 << 20) % (margin + 1)
    sizes = sizes.at[1:1 + 2 * pairs:2].set(source_of - shifted).at[2:2 + 2 * pairs:2].set(sink + shifted)
    return sizes[jax.random.permutation(jax.random.fold_in(stream_key, 2), number_of)]


def shared_out(stream_key, own, number, rows, number_of, top, reach, lean):
    sequence = jax.random.permutation(stream_key, number_of)
    packed, ordinary = load_shares(number_of, rows * top, reach, lean, True), load_shares(number_of, rows * top, reach, lean, False)
    places = jnp.arange(number_of)

    def named(lengths, turn):
        used = int((lengths > 0).sum())
        fixed = max(1, used // 4)
        passed = fixed + (places - fixed + turn * (used - fixed)) % max(1, number_of - fixed)
        return jnp.zeros((number_of,), jnp.int32).at[sequence[jnp.where(places < fixed, places, passed)]].set(jnp.asarray(lengths, jnp.int32))

    lengths = jnp.where(number % 4 == 0, named(packed, number // 4), named(ordinary, number - number // 4 - 1))
    mixed = jax.random.permutation(jax.random.fold_in(own, 3), number_of)
    source_of, taker = mixed[0:number_of // 2 * 2:2], mixed[1:number_of // 2 * 2:2]
    slack = jnp.minimum(lengths[source_of] - 1, reach - lengths[taker]) // 2
    slack = jnp.where((source_of == sequence[0]) | (taker == sequence[0]) | (lengths[taker] == 0), 0, jnp.maximum(slack, 0))
    passed = jax.random.randint(jax.random.fold_in(own, 4), (number_of // 2,), 0, 1 << 20) % (slack + 1)
    lengths = lengths.at[source_of].add(-passed).at[taker].add(passed)
    labels = jnp.searchsorted(jnp.cumsum(lengths), jnp.arange(rows * top), side="right").astype(jnp.int32)
    grid = labels.reshape(top, rows).T
    grid = grid[jax.random.permutation(jax.random.fold_in(own, 1), rows)]
    turn = jax.random.randint(jax.random.fold_in(own, 2), (rows, 1), 0, top)
    return jnp.take_along_axis(grid, (jnp.arange(top)[None, :] + turn) % top, axis=1)


def load_shares(count, total, reach, lean, full):
    loads = [(1 << 20) // math.isqrt(rank ** lean) + 1 for rank in range(1, count + 1)]
    largest = reach if full else min(reach, max(-(-total // count), total * loads[0] // sum(loads)))
    least = 1 if total - largest >= count - 1 else 0
    counts, surplus = [largest] + [least] * (count - 1), total - largest - least * (count - 1)
    while surplus > 0:
        candidates = [i for i in range(1, count) if counts[i] < largest] or [i for i in range(1, count) if counts[i] < reach]
        mass, left = sum([loads[i] for i in candidates]), surplus
        for i in candidates:
            more = min(reach - counts[i], max(1, left * loads[i] // mass), surplus)
            counts[i] = counts[i] + more
            surplus = surplus - more
    return np.array(counts)


def normal_values(key, shape, scale, limit, pieces=(), held_as=jnp.bfloat16):
    array = jax.random.normal(key, shape, jnp.float32) * scale
    if len(pieces) > 0:
        array = block_scale(key, shape, pieces, -0.22, 0.18) * array
    return jnp.clip(array, min=-limit, max=limit).astype(held_as)


def setup_inputs(seed: int = 0, part: int = 0) -> dict:
    key_of = jax.random.split(jax.random.key(seed), 10)
    own_keys = jax.random.split(jax.random.fold_in(key_of[9], part), 10)
    prompt_k = draw_prompt_k(jax.random.fold_in(jax.random.fold_in(key_of[9], part), 71), part)
    prompt_v = normal_values(own_keys[1], (N_BRANCH, PLEN, KVW), 1.0, 6.0, ((0, 16),))
    prompt_mask = draw_prompt_mask(jax.random.fold_in(jax.random.fold_in(key_of[9], part), 71), part)
    shared_kv = normal_values(own_keys[3], (NRES, RLEN, 2 * KVW), 1.0, 6.0, ((0, 16),))
    shared_len = ragged_sizes(own_keys[4], NRES, NRES * (RLEN + 1) // 2, RLEN, 2).astype(jnp.int32)
    send_pick = draw_send_pick(jax.random.fold_in(jax.random.fold_in(key_of[9], part), 71), part)
    unique_q = draw_unique_q(jax.random.fold_in(jax.random.fold_in(key_of[9], part), 71), part)
    unique_kv = draw_unique_kv(jax.random.fold_in(jax.random.fold_in(key_of[9], part), 71), part)
    unique_owner_keys = jax.random.split(jax.random.fold_in(own_keys[8], 1), ROWS // UNQ_DEV)
    unique_owner_turns = jax.random.permutation(jax.random.fold_in(own_keys[8], 3), ROWS // UNQ_DEV)
    unique_owner = jax.vmap(lambda own, number: shared_out(jax.random.fold_in(own_keys[8], 2), own, number, UNQ_DEV, N_BRANCH, 1, CAP, 2))(unique_owner_keys, unique_owner_turns).reshape((ROWS, 1))
    return {"prompt_k": prompt_k, "prompt_v": prompt_v, "prompt_mask": prompt_mask, "shared_kv": shared_kv, "shared_len": shared_len, "send_pick": send_pick, "unique_q": unique_q, "unique_kv": unique_kv, "unique_owner": unique_owner}


def attend(queries, key_rows, value_rows, allowed):
    count = queries.shape[0]
    keys_total = key_rows.shape[0]
    grouped = queries.reshape(count, KVH, GRP, HD).transpose(1, 2, 0, 3).astype(jnp.float32)
    key_heads = key_rows.reshape(keys_total, KVH, HD).transpose(1, 0, 2).astype(jnp.float32)
    value_heads = value_rows.reshape(keys_total, KVH, HD).transpose(1, 0, 2).astype(jnp.float32)
    scale = 1.0 / math.sqrt(HD)

    def one_head(operands):
        query_group, key_group, value_group = operands
        scores = jnp.einsum('gsd,kd->gsk', query_group, key_group) * scale
        scores = jnp.where(allowed[None], scores, -1e+30)
        largest = lax.optimization_barrier(jnp.max(scores, axis=-1, keepdims=True))
        weights = jnp.exp(scores - largest)
        total = lax.optimization_barrier(jnp.sum(weights, axis=-1, keepdims=True))
        probs = lax.optimization_barrier(weights.astype(jnp.bfloat16)).astype(jnp.float32)
        mixed = jnp.einsum('gsk,kd->gsd', probs, value_group)
        return (mixed / total).astype(jnp.bfloat16)
    heads = lax.map(one_head, (grouped, key_heads, value_heads))
    return heads.transpose(2, 0, 1, 3).reshape(count, QH * HD)

def reference(prompt_k, prompt_v, prompt_mask, shared_kv, shared_len, send_pick, unique_q, unique_kv, unique_owner):
    owner_of = unique_owner[:, 0].astype(jnp.int32)
    positions = jnp.arange(ROWS, dtype=jnp.int32)
    source = positions // UNQ_DEV
    grid_owner = owner_of.reshape(N_BRANCH, UNQ_DEV)
    in_device = jnp.arange(UNQ_DEV, dtype=jnp.int32)
    earlier = (grid_owner[:, :, None] == grid_owner[:, None, :]) & (in_device[None, None, :] < in_device[None, :, None])
    rank = lax.optimization_barrier(jnp.sum(earlier.astype(jnp.int32), axis=2)).reshape(ROWS).astype(jnp.int32)
    slot_index = (source * CAP + rank).astype(jnp.int32)
    width = N_BRANCH * CAP
    query_slots = jnp.zeros((N_BRANCH, width, QW), jnp.bfloat16).at[owner_of, slot_index].set(unique_q)
    pair_slots = jnp.zeros((N_BRANCH, width, 2 * KVW), jnp.bfloat16).at[owner_of, slot_index].set(unique_kv)
    live_slots = jnp.zeros((N_BRANCH, width), jnp.int32).at[owner_of, slot_index].set(1)
    by_owner = shared_kv.reshape(N_BRANCH, RES_DEV, RLEN, 2 * KVW)
    len_by_owner = shared_len.reshape(N_BRANCH, RES_DEV)
    owners = jnp.arange(N_BRANCH, dtype=jnp.int32)
    within = jnp.arange(RLEN, dtype=jnp.int32)
    slot_range = jnp.arange(width, dtype=jnp.int32)
    causal = slot_range[None, :] <= slot_range[:, None]

    def one_branch(branch_id):
        picked = send_pick[:, branch_id]
        safe = jnp.maximum(picked, 0).astype(jnp.int32)
        fetched = by_owner[owners, safe].reshape(N_BRANCH * RLEN, 2 * KVW)
        live_len = jnp.where(picked >= 0, len_by_owner[owners, safe], 0)
        shared_ok = (within[None, :] < live_len[:, None]).reshape(N_BRANCH * RLEN)
        block_ok = jnp.repeat(prompt_mask[branch_id] > 0, PB)
        unique_ok = causal & (live_slots[branch_id] > 0)[None, :]
        allowed = jnp.concatenate([jnp.broadcast_to(block_ok[None], (width, PLEN)), jnp.broadcast_to(shared_ok[None], (width, N_BRANCH * RLEN)), unique_ok], axis=1)
        pairs = pair_slots[branch_id]
        key_rows = jnp.concatenate([prompt_k[branch_id], fetched[:, :KVW], pairs[:, :KVW]], axis=0)
        value_rows = jnp.concatenate([prompt_v[branch_id], fetched[:, KVW:], pairs[:, KVW:]], axis=0)
        return attend(query_slots[branch_id], key_rows, value_rows, allowed)
    results = lax.map(one_branch, owners)
    return results[owner_of, slot_index]
```

```python
import functools
import math

import jax
import jax.numpy as jnp
from jax import lax
from jax.experimental import pallas as pl
from jax.experimental.pallas import tpu as pltpu
from jax.sharding import PartitionSpec as P

HD = 128
GRP = 8
NEG = -1e30
MESH = pl.DeviceIdType.MESH


def kernel(
    n, across, cap, rlen, res, heads,
    row_of, slot_of, q_ref, kv_ref, meta_ref, pbias_ref, shared_ref, pk_hbm, pv_hbm,
    out_ref,
    pk, pv, xs, xr, mr, gath, tail, kslot, uni, acc, stat, ox, orx,
    psem, lsem, xsend, xrecv, msend, mrecv, gsend, grecv, rsend, rrecv,
):
    me = lax.axis_index("branch")
    kvh = heads // GRP
    pairs = kvh // 2
    width = n * cap
    rows = width * GRP
    kvw = kvh * HD
    line = n // (2 * across)
    core = lax.rem(me, 2)
    chip = me // 2
    y = lax.rem(chip, across)
    z = chip // across
    sibling = me + 1 - 2 * core
    tail_n = tail.shape[0]
    scale = math.log2(math.e) / math.sqrt(HD)

    copy_k = pltpu.make_async_copy(pk_hbm.at[0], pk, psem.at[0])
    copy_v = pltpu.make_async_copy(pv_hbm.at[0], pv, psem.at[1])
    copy_k.start()
    copy_v.start()

    barrier = pltpu.get_barrier_semaphore()

    def greet(i, c):
        pl.semaphore_signal(
            barrier, inc=1, device_id={"branch": lax.rem(me + i, n)}, device_id_type=MESH
        )
        return c

    lax.fori_loop(1, n, greet, 0)

    def place(j, c):
        row = row_of[j]
        xs[j, :heads] = q_ref[row]
        xs[j, heads:] = kv_ref[row]
        return c

    lax.fori_loop(0, width, place, 0)
    pl.semaphore_wait(barrier, n - 1)

    def ship(src, source, e, target, way):
        return pltpu.make_async_remote_copy(
            src_ref=src,
            dst_ref=gath.at[source, e],
            send_sem=gsend.at[way, source * res + e],
            recv_sem=grecv.at[source * res + e],
            device_id={"branch": target},
            device_id_type=MESH,
        )

    def member(zz, yy, cc):
        return (zz * across + yy) * 2 + cc

    def spread(zs, e, first, act):
        source = member(zs, y, core)
        src = shared_ref.at[e] if first else gath.at[source, e]

        @pl.when(jnp.logical_and(zs <= z, z + 1 < line))
        def _():
            act(ship(src, source, e, member(lax.rem(z + 1, line), y, core), 0))

        @pl.when(jnp.logical_and(zs >= z, z >= 1))
        def _():
            act(ship(src, source, e, member(lax.rem(z + line - 1, line), y, core), 1))

        for d in range(1, across):
            act(ship(src, source, e, member(z, lax.rem(y + d, across), core), 1 + d))
        act(ship(src, source, e, sibling, 1 + across))

    def arrived(source, e):
        ship(gath.at[source, e], source, e, sibling, 0).wait_recv()

    begin = lambda copy: copy.start()
    finish = lambda copy: copy.wait_send()

    def on_line(t, act, waits):
        for up in (0, 1):
            zs = z - t if up == 0 else z + t
            ok = zs >= 0 if up == 0 else zs < line

            @pl.when(ok)
            def _():
                zc = lax.rem(zs + line, line)
                for e in range(res):
                    if waits:
                        arrived(member(zc, y, core), e)
                    spread(zc, e, False, act)

    def cross(zs, act, waits):
        for d in range(1, across):
            source = member(zs, lax.rem(y + d, across), core)
            for e in range(res):
                if waits:
                    arrived(source, e)
                act(ship(gath.at[source, e], source, e, sibling, 1 + across))

    def off_line(t, act, waits):
        @pl.when(z - t >= 0)
        def _():
            cross(lax.rem(z - t + line, line), act, waits)

        @pl.when(jnp.logical_and(z + t < line, t > 0))
        def _():
            cross(lax.rem(z + t, line), act, waits)

    def relay(t, c):
        on_line(t, begin, True)
        off_line(t - 1, begin, True)
        return c

    for e in range(res):
        spread(z, e, True, begin)

    def part(ref, b):
        return ref.at[pl.ds(b * cap, cap)]

    def x_copy(i, b, at):
        return pltpu.make_async_remote_copy(
            src_ref=part(xs, b), dst_ref=part(xr, at), send_sem=xsend.at[i], recv_sem=xrecv.at[i],
            device_id={"branch": b}, device_id_type=MESH,
        )

    def m_copy(i, b, at):
        return pltpu.make_async_remote_copy(
            src_ref=meta_ref.at[b], dst_ref=mr.at[at], send_sem=msend.at[i], recv_sem=mrecv.at[i],
            device_id={"branch": b}, device_id_type=MESH,
        )

    def send_x(i, c):
        b = lax.rem(me + i, n)
        x_copy(i, b, me).start()
        m_copy(i, b, me).start()
        return c

    lax.fori_loop(1, n, send_x, 0)
    own_x = pltpu.make_async_copy(part(xs, me), part(xr, me), lsem.at[0])
    own_m = pltpu.make_async_copy(meta_ref.at[me], mr.at[me], lsem.at[1])
    own_x.start()
    own_m.start()
    gath[me] = shared_ref[...]
    tail[...] = jnp.zeros_like(tail)

    def take_x(i, c):
        b = lax.rem(me + n - i, n)
        x_copy(i, b, b).wait_recv()
        m_copy(i, b, b).wait_recv()
        return c

    lax.fori_loop(1, n, take_x, 0)
    own_x.wait()
    own_m.wait()
    copy_k.wait()
    copy_v.wait()

    def queries(p):
        both = xr[:, pl.ds(p * 2 * GRP, 2 * GRP), :].astype(jnp.float32)
        return [
            both[:, k * GRP : (k + 1) * GRP].reshape(rows, HD).astype(jnp.bfloat16)
            for k in range(2)
        ]

    def scores(q, k):
        return lax.dot_general(q, k, (((1,), (1,)), ((), ())), preferred_element_type=jnp.float32)

    half = lax.broadcasted_iota(jnp.int32, (rows, HD), 1) < HD // 2

    def prompt_pair(p):
        for k, q in enumerate(queries(p)):
            h = 2 * p + k
            cols = slice(h * HD, (h + 1) * HD)
            s = scores(q, pk[:, cols]) * scale + pbias_ref[...]
            m = jnp.max(s, axis=-1, keepdims=True)
            w = jnp.exp2(s - m)
            stat[h] = jnp.where(half, m, jnp.sum(w, axis=-1, keepdims=True))
            acc[h] = jnp.dot(
                w.astype(jnp.bfloat16), pv[:, cols], preferred_element_type=jnp.float32
            )

    cuts = [1 + (line - 1) * p // pairs for p in range(pairs + 1)]
    for p in range(pairs):
        prompt_pair(p)
        if cuts[p] < cuts[p + 1]:
            lax.fori_loop(cuts[p], cuts[p + 1], relay, 0)
    off_line(line - 1, begin, True)

    uni[...] = xr[:, heads:, :].astype(jnp.float32).reshape(width * 2 * kvh, HD)
    for j in range(2 * kvh):
        tail[n * rlen : n * rlen + width, j * HD : (j + 1) * HD] = uni[
            pl.ds(j, width, stride=2 * kvh), :
        ].astype(jnp.bfloat16)
    col = lax.broadcasted_iota(jnp.int32, (1, tail_n), 1)

    def limits(s, carry):
        length, live = carry
        meta = mr[s]
        length = jnp.where(col // rlen == s, meta[1:2, 0:1], length)
        for k in range(cap):
            live = jnp.where(col == n * rlen + s * cap + k, meta[2 + k : 3 + k, 0:1], live)
        return length, live

    zero = jnp.zeros((1, tail_n), jnp.int32)
    length, live = lax.fori_loop(0, n, limits, (zero, zero))
    shared_ok = jnp.logical_and(col < n * rlen, lax.rem(col, rlen) < length)
    kslot[...] = jnp.where(shared_ok, -1, jnp.where(live > 0, col - n * rlen, width))
    row_slot = lax.broadcasted_iota(jnp.int32, (rows, 1), 0) // GRP

    def far(i, c):
        for yy in range(across):
            source = member(i, yy, 1 - core)
            for e in range(res):
                arrived(source, e)
        return c

    lax.fori_loop(0, line, far, 0)

    def choose(t, c):
        two = []
        for s in (2 * t, 2 * t + 1):
            pick = mr[s][0:1, 0:1]
            chosen = gath[s, 0].astype(jnp.float32)
            for e in range(1, res):
                chosen = jnp.where(pick == e, gath[s, e].astype(jnp.float32), chosen)
            two.append(chosen)
        tail[pl.ds(pl.multiple_of(t * 2 * rlen, 16), 2 * rlen), :] = jnp.concatenate(
            two, axis=0
        ).astype(jnp.bfloat16)
        return c

    lax.fori_loop(0, n // 2, choose, 0)

    def tail_pair(p):
        done = []
        for k, q in enumerate(queries(p)):
            h = 2 * p + k
            keys = tail[:, h * HD : (h + 1) * HD]
            values = tail[:, kvw + h * HD : kvw + (h + 1) * HD]
            s = jnp.where(kslot[...] <= row_slot, scores(q, keys) * scale, NEG)
            before = stat[h][:, :1]
            m = jnp.maximum(before, jnp.max(s, axis=-1, keepdims=True))
            w = jnp.exp2(s - m)
            keep = jnp.exp2(before - m)
            total = stat[h][:, HD // 2 : HD // 2 + 1] * keep + jnp.sum(w, axis=-1, keepdims=True)
            mixed = acc[h] * keep + jnp.dot(
                w.astype(jnp.bfloat16), values, preferred_element_type=jnp.float32
            )
            done.append((mixed / total).reshape(width, GRP, HD))
        ox[:, p * 2 * GRP : (p + 1) * 2 * GRP, :] = jnp.concatenate(done, axis=1).astype(
            jnp.bfloat16
        )

    def r_copy(p, i, b, at):
        cut = pl.ds(p * 2 * GRP, 2 * GRP)
        return pltpu.make_async_remote_copy(
            src_ref=ox.at[pl.ds(b * cap, cap), cut], dst_ref=orx.at[pl.ds(at * cap, cap), cut],
            send_sem=rsend.at[p, i], recv_sem=rrecv.at[p, i],
            device_id={"branch": b}, device_id_type=MESH,
        )

    def give_back(p):
        def one(i, c):
            r_copy(p, i, lax.rem(me + i, n), me).start()
            return c

        lax.fori_loop(1, n, one, 0)

    for p in range(pairs):
        tail_pair(p)
        if p:
            give_back(p - 1)
    give_back(pairs - 1)
    own_r = pltpu.make_async_copy(part(ox, me), part(orx, me), lsem.at[2])
    own_r.start()

    def sent(i, c):
        b = lax.rem(me + i, n)
        x_copy(i, b, me).wait_send()
        m_copy(i, b, me).wait_send()
        return c

    lax.fori_loop(1, n, sent, 0)
    for e in range(res):
        spread(z, e, True, finish)

    def relayed(t, c):
        on_line(t, finish, False)
        off_line(t - 1, finish, False)
        return c

    lax.fori_loop(1, line, relayed, 0)
    off_line(line - 1, finish, False)

    def returned(i, c):
        for p in range(pairs):
            r_copy(p, i, lax.rem(me + n - i, n), lax.rem(me + n - i, n)).wait_recv()
        return c

    lax.fori_loop(1, n, returned, 0)
    own_r.wait()

    def collect(j, c):
        out_ref[j] = orx[slot_of[j]]
        return c

    lax.fori_loop(0, out_ref.shape[0], collect, 0)

    def gone(i, c):
        for p in range(pairs):
            r_copy(p, i, lax.rem(me + i, n), me).wait_send()
        return c

    lax.fori_loop(1, n, gone, 0)


def body(
    across, prompt_k, prompt_v, prompt_mask, shared_kv, shared_len, send_pick,
    unique_q, unique_kv, unique_owner,
):
    n = lax.axis_size("branch")
    rows = unique_q.shape[0]
    cap = 2 * rows // n
    width = n * cap
    res, rlen = shared_kv.shape[:2]
    heads = unique_q.shape[1] // HD
    kvh = unique_kv.shape[1] // (2 * HD)
    plen = prompt_k.shape[1]
    owner = unique_owner[:, 0]
    order = jnp.arange(rows, dtype=jnp.int32)
    earlier = (owner[:, None] == owner[None, :]) & (order[None, :] < order[:, None])
    slot_of = owner * cap + jnp.sum(earlier.astype(jnp.int32), axis=1)
    matches = jnp.arange(width, dtype=jnp.int32)[:, None] == slot_of[None, :]
    row_of = jnp.sum(jnp.where(matches, order[None, :], 0), axis=1)
    live = jnp.any(matches, axis=1).astype(jnp.int32).reshape(n, cap)
    pick = send_pick[0]
    length = jnp.zeros_like(pick)
    for e in range(res):
        length = jnp.where(pick == e, shared_len[e], length)
    meta = jnp.concatenate([pick[:, None], length[:, None], live], axis=1)
    meta = jnp.broadcast_to(meta[:, :, None], meta.shape + (HD,))
    block = plen // prompt_mask.shape[1]
    pbias = jnp.where(jnp.repeat(prompt_mask > 0, block, axis=1), 0.0, NEG).astype(jnp.float32)
    tail_n = -(-(n * rlen + width) // 128) * 128
    qrows = width * GRP
    vmem = pl.BlockSpec(memory_space=pltpu.VMEM)
    smem = pl.BlockSpec(memory_space=pltpu.SMEM)
    anyp = pl.BlockSpec(memory_space=pl.ANY)
    bf, f32 = jnp.bfloat16, jnp.float32
    dma = pltpu.SemaphoreType.DMA
    out = pl.pallas_call(
        functools.partial(kernel, n, across, cap, rlen, res, heads),
        out_shape=jax.ShapeDtypeStruct((rows, heads, HD), bf),
        in_specs=[smem, smem, vmem, vmem, vmem, vmem, vmem, anyp, anyp],
        out_specs=vmem,
        scratch_shapes=[
            pltpu.VMEM(prompt_k.shape[1:], bf),
            pltpu.VMEM(prompt_v.shape[1:], bf),
            pltpu.VMEM((width, heads + 2 * kvh, HD), bf),
            pltpu.VMEM((width, heads + 2 * kvh, HD), bf),
            pltpu.VMEM((n,) + meta.shape[1:], jnp.int32),
            pltpu.VMEM((n,) + shared_kv.shape, bf),
            pltpu.VMEM((tail_n, 2 * kvh * HD), bf),
            pltpu.VMEM((1, tail_n), jnp.int32),
            pltpu.VMEM((width * 2 * kvh, HD), f32),
            pltpu.VMEM((kvh, qrows, HD), f32),
            pltpu.VMEM((kvh, qrows, HD), f32),
            pltpu.VMEM((width, heads, HD), bf),
            pltpu.VMEM((width, heads, HD), bf),
            dma((2,)),
            dma((3,)),
            dma((n,)),
            dma((n,)),
            dma((n,)),
            dma((n,)),
            dma((2 + across, n * res)),
            dma((n * res,)),
            dma((kvh // 2, n)),
            dma((kvh // 2, n)),
        ],
        compiler_params=pltpu.CompilerParams(
            collective_id=0, has_side_effects=True, vmem_limit_bytes=62 * 1024 * 1024
        ),
    )(
        row_of, slot_of, unique_q.reshape(rows, heads, HD),
        unique_kv.reshape(rows, 2 * kvh, HD), meta, pbias, shared_kv, prompt_k, prompt_v,
    )
    return out.reshape(rows, heads * HD)


def chips_across(mesh):
    devices = mesh.devices.reshape(-1, mesh.shape["branch"])[0]
    try:
        places = [tuple(d.coords) for d in devices[::2]]
    except (AttributeError, TypeError):
        return 1
    return sum(1 for p in places if p[2] == places[0][2])


def solution(mesh):
    spec1, spec2, spec3 = (P(("groups", "branch"), *(None,) * k) for k in range(3))
    in_specs = (spec3, spec3, spec2, spec3, spec1, spec2, spec2, spec2, spec2)
    return jax.shard_map(
        functools.partial(body, chips_across(mesh)),
        mesh=mesh, in_specs=in_specs, out_specs=spec2, check_vma=False,
    )
```

```python
import functools
import math

import jax
import jax.numpy as jnp
from jax import lax
from jax.experimental import pallas as pl
from jax.experimental.pallas import tpu as pltpu
from jax.sharding import PartitionSpec as P

HD = 128
GRP = 8
NEG = -1e30
MESH = pl.DeviceIdType.MESH


def kernel(
    n, across, cap, rlen, res, heads,
    owner_ref, pick_ref, len_ref, mask_ref, q_ref, kv_ref, shared_ref, pk_hbm, pv_hbm,
    out_ref,
    pk, pv, flat, by_row, slot_of, pbias, meta_ref, xs, xr, mr, gath, tail, kslot, acc, stat, ox, orx,
    psem, lsem, xsend, xrecv, msend, mrecv, gsend, grecv, rsend, rrecv,
):
    me = lax.axis_index("branch")
    kvh = heads // GRP
    pairs = kvh // 2
    width = n * cap
    rows = width * GRP
    kvw = kvh * HD
    line = n // (2 * across)
    core = lax.rem(me, 2)
    chip = me // 2
    y = lax.rem(chip, across)
    z = chip // across
    sibling = me + 1 - 2 * core
    tail_n = tail.shape[0]
    scale = math.log2(math.e) / math.sqrt(HD)

    copy_k = pltpu.make_async_copy(pk_hbm.at[0], pk, psem.at[0])
    copy_v = pltpu.make_async_copy(pv_hbm.at[0], pv, psem.at[1])
    copy_k.start()
    copy_v.start()

    barrier = pltpu.get_barrier_semaphore()

    def greet(i, c):
        pl.semaphore_signal(
            barrier, inc=1, device_id={"branch": lax.rem(me + i, n)}, device_id_type=MESH
        )
        return c

    lax.fori_loop(1, n, greet, 0)

    count = q_ref.shape[0]
    per = heads + 2 * kvh
    some = min(count, 16)
    for r in range(0, count, some):
        for h in range(per):
            ref, g = (q_ref, h) if h < heads else (kv_ref, h - heads)
            flat[pl.ds(h, some, stride=per), :] = ref[
                r : r + some, g * HD : (g + 1) * HD
            ].astype(jnp.float32)
        for i in range(some):
            by_row[r + i] = flat[i * per : (i + 1) * per].astype(jnp.bfloat16)

    def number(j, c):
        mine = owner_ref[j]
        rank = lax.fori_loop(
            0, j, lambda i, r: r + jnp.where(owner_ref[i] == mine, 1, 0), jnp.int32(0)
        )
        slot_of[j] = mine * cap + rank
        return c

    lax.fori_loop(0, count, number, 0)

    def place(b, c):
        def scan(i, found):
            hit = owner_ref[i] == b
            rows_at, seen = found[:cap], found[cap]
            rows_at = [
                jnp.where(jnp.logical_and(hit, seen == k), i, r) for k, r in enumerate(rows_at)
            ]
            return (*rows_at, seen + jnp.where(hit, 1, 0))

        found = lax.fori_loop(0, count, scan, (jnp.int32(0),) * (cap + 1))
        pick = pick_ref[0, b]
        length = jnp.int32(0)
        for e in range(res):
            length = jnp.where(pick == e, len_ref[e], length)
        meta_ref[b, 0:1] = jnp.full((1, HD), pick, jnp.int32)
        meta_ref[b, 1:2] = jnp.full((1, HD), length, jnp.int32)
        for k in range(cap):
            xs[b * cap + k] = by_row[found[k]]
            meta_ref[b, 2 + k : 3 + k] = jnp.full(
                (1, HD), jnp.where(found[cap] > k, 1, 0), jnp.int32
            )
        return c

    lax.fori_loop(0, n, place, 0)
    blocks = mask_ref.shape[1]
    block = pk.shape[0] // blocks
    for g in range(blocks):
        pbias[:, g * block : (g + 1) * block] = jnp.full(
            (1, block), jnp.where(mask_ref[0, g] > 0, 0.0, NEG), jnp.float32
        )
    pl.semaphore_wait(barrier, n - 1)

    def ship(src, source, e, target, way):
        return pltpu.make_async_remote_copy(
            src_ref=src,
            dst_ref=gath.at[source, e],
            send_sem=gsend.at[way, source * res + e],
            recv_sem=grecv.at[source * res + e],
            device_id={"branch": target},
            device_id_type=MESH,
        )

    def member(zz, yy, cc):
        return (zz * across + yy) * 2 + cc

    def spread(zs, e, first, act):
        source = member(zs, y, core)
        src = shared_ref.at[e] if first else gath.at[source, e]

        @pl.when(jnp.logical_and(zs <= z, z + 1 < line))
        def _():
            act(ship(src, source, e, member(lax.rem(z + 1, line), y, core), 0))

        @pl.when(jnp.logical_and(zs >= z, z >= 1))
        def _():
            act(ship(src, source, e, member(lax.rem(z + line - 1, line), y, core), 1))

        for d in range(1, across):
            act(ship(src, source, e, member(z, lax.rem(y + d, across), core), 1 + d))
        act(ship(src, source, e, sibling, 1 + across))

    def arrived(source, e):
        ship(gath.at[source, e], source, e, sibling, 0).wait_recv()

    begin = lambda copy: copy.start()
    finish = lambda copy: copy.wait_send()

    def on_line(t, act, waits):
        for up in (0, 1):
            zs = z - t if up == 0 else z + t
            ok = zs >= 0 if up == 0 else zs < line

            @pl.when(ok)
            def _():
                zc = lax.rem(zs + line, line)
                for e in range(res):
                    if waits:
                        arrived(member(zc, y, core), e)
                    spread(zc, e, False, act)

    def cross(zs, act, waits):
        for d in range(1, across):
            source = member(zs, lax.rem(y + d, across), core)
            for e in range(res):
                if waits:
                    arrived(source, e)
                act(ship(gath.at[source, e], source, e, sibling, 1 + across))

    def off_line(t, act, waits):
        @pl.when(z - t >= 0)
        def _():
            cross(lax.rem(z - t + line, line), act, waits)

        @pl.when(jnp.logical_and(z + t < line, t > 0))
        def _():
            cross(lax.rem(z + t, line), act, waits)

    def relay(t, c):
        on_line(t, begin, True)
        off_line(t - 1, begin, True)
        return c


    def part(ref, b):
        return ref.at[pl.ds(b * cap, cap)]

    def x_copy(i, b, at):
        return pltpu.make_async_remote_copy(
            src_ref=part(xs, b), dst_ref=part(xr, at), send_sem=xsend.at[i], recv_sem=xrecv.at[i],
            device_id={"branch": b}, device_id_type=MESH,
        )

    def m_copy(i, b, at):
        return pltpu.make_async_remote_copy(
            src_ref=meta_ref.at[b], dst_ref=mr.at[at], send_sem=msend.at[i], recv_sem=mrecv.at[i],
            device_id={"branch": b}, device_id_type=MESH,
        )

    def send_x(i, c):
        b = lax.rem(me + i, n)
        x_copy(i, b, me).start()
        m_copy(i, b, me).start()
        return c

    lax.fori_loop(1, n, send_x, 0)
    for e in range(res):
        spread(z, e, True, begin)
    own_x = pltpu.make_async_copy(part(xs, me), part(xr, me), lsem.at[0])
    own_m = pltpu.make_async_copy(meta_ref.at[me], mr.at[me], lsem.at[1])
    own_x.start()
    own_m.start()
    gath[me] = shared_ref[...]
    tail[...] = jnp.zeros_like(tail)

    def take_x(i, c):
        b = lax.rem(me + n - i, n)
        x_copy(i, b, b).wait_recv()
        m_copy(i, b, b).wait_recv()
        return c

    lax.fori_loop(1, n, take_x, 0)
    own_x.wait()
    own_m.wait()
    copy_k.wait()
    copy_v.wait()

    def queries(p):
        both = xr[:, pl.ds(p * 2 * GRP, 2 * GRP), :].astype(jnp.float32)
        return [
            both[:, k * GRP : (k + 1) * GRP].reshape(rows, HD).astype(jnp.bfloat16)
            for k in range(2)
        ]

    def scores(q, k):
        return lax.dot_general(q, k, (((1,), (1,)), ((), ())), preferred_element_type=jnp.float32)

    half = lax.broadcasted_iota(jnp.int32, (rows, HD), 1) < HD // 2

    def prompt_pair(p):
        for k, q in enumerate(queries(p)):
            h = 2 * p + k
            cols = slice(h * HD, (h + 1) * HD)
            s = scores(q, pk[:, cols]) * scale + pbias[...]
            m = jnp.max(s, axis=-1, keepdims=True)
            w = jnp.exp2(s - m)
            stat[h] = jnp.where(half, m, jnp.sum(w, axis=-1, keepdims=True))
            acc[h] = jnp.dot(
                w.astype(jnp.bfloat16), pv[:, cols], preferred_element_type=jnp.float32
            )

    cuts = [1 + (line - 1) * p // pairs for p in range(pairs + 1)]
    for p in range(pairs):
        prompt_pair(p)
        if cuts[p] < cuts[p + 1]:
            lax.fori_loop(cuts[p], cuts[p + 1], relay, 0)
    off_line(line - 1, begin, True)

    flat[: width * 2 * kvh] = (
        xr[:, heads:, :].astype(jnp.float32).reshape(width * 2 * kvh, HD)
    )
    for j in range(2 * kvh):
        tail[n * rlen : n * rlen + width, j * HD : (j + 1) * HD] = flat[
            pl.ds(j, width, stride=2 * kvh), :
        ].astype(jnp.bfloat16)
    col = lax.broadcasted_iota(jnp.int32, (1, tail_n), 1)

    def limits(s, carry):
        length, live = carry
        meta = mr[s]
        length = jnp.where(col // rlen == s, meta[1:2, 0:1], length)
        for k in range(cap):
            live = jnp.where(col == n * rlen + s * cap + k, meta[2 + k : 3 + k, 0:1], live)
        return length, live

    zero = jnp.zeros((1, tail_n), jnp.int32)
    length, live = lax.fori_loop(0, n, limits, (zero, zero))
    shared_ok = jnp.logical_and(col < n * rlen, lax.rem(col, rlen) < length)
    kslot[...] = jnp.where(shared_ok, -1, jnp.where(live > 0, col - n * rlen, width))
    row_slot = lax.broadcasted_iota(jnp.int32, (rows, 1), 0) // GRP

    def far(i, c):
        for yy in range(across):
            source = member(i, yy, 1 - core)
            for e in range(res):
                arrived(source, e)
        return c

    lax.fori_loop(0, line, far, 0)

    def choose(t, c):
        two = []
        for s in (2 * t, 2 * t + 1):
            pick = mr[s][0:1, 0:1]
            chosen = gath[s, 0].astype(jnp.float32)
            for e in range(1, res):
                chosen = jnp.where(pick == e, gath[s, e].astype(jnp.float32), chosen)
            two.append(chosen)
        tail[pl.ds(pl.multiple_of(t * 2 * rlen, 16), 2 * rlen), :] = jnp.concatenate(
            two, axis=0
        ).astype(jnp.bfloat16)
        return c

    lax.fori_loop(0, n // 2, choose, 0)

    def tail_pair(p):
        done = []
        for k, q in enumerate(queries(p)):
            h = 2 * p + k
            keys = tail[:, h * HD : (h + 1) * HD]
            values = tail[:, kvw + h * HD : kvw + (h + 1) * HD]
            s = jnp.where(kslot[...] <= row_slot, scores(q, keys) * scale, NEG)
            before = stat[h][:, :1]
            m = jnp.maximum(before, jnp.max(s, axis=-1, keepdims=True))
            w = jnp.exp2(s - m)
            keep = jnp.exp2(before - m)
            total = stat[h][:, HD // 2 : HD // 2 + 1] * keep + jnp.sum(w, axis=-1, keepdims=True)
            mixed = acc[h] * keep + jnp.dot(
                w.astype(jnp.bfloat16), values, preferred_element_type=jnp.float32
            )
            done.append((mixed / total).reshape(width, GRP, HD))
        ox[:, p * 2 * GRP : (p + 1) * 2 * GRP, :] = jnp.concatenate(done, axis=1).astype(
            jnp.bfloat16
        )

    def r_copy(p, i, b, at):
        cut = pl.ds(p * 2 * GRP, 2 * GRP)
        return pltpu.make_async_remote_copy(
            src_ref=ox.at[pl.ds(b * cap, cap), cut], dst_ref=orx.at[pl.ds(at * cap, cap), cut],
            send_sem=rsend.at[p, i], recv_sem=rrecv.at[p, i],
            device_id={"branch": b}, device_id_type=MESH,
        )

    def give_back(p):
        def one(i, c):
            r_copy(p, i, lax.rem(me + i, n), me).start()
            return c

        lax.fori_loop(1, n, one, 0)

    for p in range(pairs):
        tail_pair(p)
        if p:
            give_back(p - 1)
    give_back(pairs - 1)
    own_r = pltpu.make_async_copy(part(ox, me), part(orx, me), lsem.at[2])
    own_r.start()

    def sent(i, c):
        b = lax.rem(me + i, n)
        x_copy(i, b, me).wait_send()
        m_copy(i, b, me).wait_send()
        return c

    lax.fori_loop(1, n, sent, 0)
    for e in range(res):
        spread(z, e, True, finish)

    def relayed(t, c):
        on_line(t, finish, False)
        off_line(t - 1, finish, False)
        return c

    lax.fori_loop(1, line, relayed, 0)
    off_line(line - 1, finish, False)

    def returned(i, c):
        for p in range(pairs):
            r_copy(p, i, lax.rem(me + n - i, n), lax.rem(me + n - i, n)).wait_recv()
        return c

    lax.fori_loop(1, n, returned, 0)
    own_r.wait()

    for r in range(0, count, some):
        for i in range(some):
            flat[i * heads : (i + 1) * heads] = orx[slot_of[r + i]].astype(jnp.float32)
        for h in range(heads):
            out_ref[r : r + some, h * HD : (h + 1) * HD] = flat[
                pl.ds(h, some, stride=heads), :
            ].astype(jnp.bfloat16)

    def gone(i, c):
        for p in range(pairs):
            r_copy(p, i, lax.rem(me + i, n), me).wait_send()
        return c

    lax.fori_loop(1, n, gone, 0)


def body(
    across, prompt_k, prompt_v, prompt_mask, shared_kv, shared_len, send_pick,
    unique_q, unique_kv, unique_owner,
):
    n = lax.axis_size("branch")
    rows = unique_q.shape[0]
    cap = 2 * rows // n
    width = n * cap
    res, rlen = shared_kv.shape[:2]
    heads = unique_q.shape[1] // HD
    kvh = unique_kv.shape[1] // (2 * HD)
    plen = prompt_k.shape[1]
    tail_n = -(-(n * rlen + width) // 128) * 128
    qrows = width * GRP
    vmem = pl.BlockSpec(memory_space=pltpu.VMEM)
    smem = pl.BlockSpec(memory_space=pltpu.SMEM)
    anyp = pl.BlockSpec(memory_space=pl.ANY)
    bf, f32 = jnp.bfloat16, jnp.float32
    dma = pltpu.SemaphoreType.DMA
    out = pl.pallas_call(
        functools.partial(kernel, n, across, cap, rlen, res, heads),
        out_shape=jax.ShapeDtypeStruct((rows, heads * HD), bf),
        in_specs=[smem, smem, smem, smem, vmem, vmem, vmem, anyp, anyp],
        out_specs=vmem,
        scratch_shapes=[
            pltpu.VMEM(prompt_k.shape[1:], bf),
            pltpu.VMEM(prompt_v.shape[1:], bf),
            pltpu.VMEM((max(min(rows, 16) * (heads + 2 * kvh), width * 2 * kvh), HD), f32),
            pltpu.VMEM((rows, heads + 2 * kvh, HD), bf),
            pltpu.SMEM((rows,), jnp.int32),
            pltpu.VMEM((1, plen), f32),
            pltpu.VMEM((n, 2 + cap, HD), jnp.int32),
            pltpu.VMEM((width, heads + 2 * kvh, HD), bf),
            pltpu.VMEM((width, heads + 2 * kvh, HD), bf),
            pltpu.VMEM((n, 2 + cap, HD), jnp.int32),
            pltpu.VMEM((n,) + shared_kv.shape, bf),
            pltpu.VMEM((tail_n, 2 * kvh * HD), bf),
            pltpu.VMEM((1, tail_n), jnp.int32),
            pltpu.VMEM((kvh, qrows, HD), f32),
            pltpu.VMEM((kvh, qrows, HD), f32),
            pltpu.VMEM((width, heads, HD), bf),
            pltpu.VMEM((width, heads, HD), bf),
            dma((2,)),
            dma((3,)),
            dma((n,)),
            dma((n,)),
            dma((n,)),
            dma((n,)),
            dma((2 + across, n * res)),
            dma((n * res,)),
            dma((kvh // 2, n)),
            dma((kvh // 2, n)),
        ],
        compiler_params=pltpu.CompilerParams(
            collective_id=0, has_side_effects=True, vmem_limit_bytes=67043328
        ),
    )(
        unique_owner.reshape(rows), send_pick, shared_len, prompt_mask,
        unique_q, unique_kv, shared_kv, prompt_k, prompt_v,
    )
    return out


def chips_across(mesh):
    devices = mesh.devices.reshape(-1, mesh.shape["branch"])[0]
    try:
        places = [tuple(d.coords) for d in devices[::2]]
    except (AttributeError, TypeError):
        return 1
    return sum(1 for p in places if p[2] == places[0][2])


def solution(mesh):
    spec1, spec2, spec3 = (P(("groups", "branch"), *(None,) * k) for k in range(3))
    in_specs = (spec3, spec3, spec2, spec3, spec1, spec2, spec2, spec2, spec2)
    return jax.shard_map(
        functools.partial(body, chips_across(mesh)),
        mesh=mesh, in_specs=in_specs, out_specs=spec2, check_vma=False,
    )
```

```python
import functools
import math

import jax
import jax.numpy as jnp
from jax import lax
from jax.experimental import pallas as pl
from jax.experimental.pallas import tpu as pltpu
from jax.sharding import PartitionSpec as P

HD = 128
GRP = 8
NEG = -1e30
MESH = pl.DeviceIdType.MESH


def kernel(
    n, across, cap, rlen, res, heads,
    owner_ref, pick_ref, len_ref, mask_ref, q_ref, kv_ref, shared_ref, pk_hbm, pv_hbm,
    out_ref,
    pk, pv, flat, by_row, slot_of, pbias, meta_ref, xs, xr, mr, gath, tail, kslot, acc, stat, ox, orx,
    psem, lsem, xsend, xrecv, msend, mrecv, gsend, grecv, rsend, rrecv,
):
    me = lax.axis_index("branch")
    kvh = heads // GRP
    pairs = kvh // 2
    width = n * cap
    rows = width * GRP
    kvw = kvh * HD
    line = n // (2 * across)
    core = lax.rem(me, 2)
    chip = me // 2
    y = lax.rem(chip, across)
    z = chip // across
    sibling = me + 1 - 2 * core
    tail_n = tail.shape[0]
    scale = math.log2(math.e) / math.sqrt(HD)

    copy_k = pltpu.make_async_copy(pk_hbm.at[0], pk, psem.at[0])
    copy_v = pltpu.make_async_copy(pv_hbm.at[0], pv, psem.at[1])
    copy_k.start()
    copy_v.start()

    barrier = pltpu.get_barrier_semaphore()

    def greet(i, c):
        pl.semaphore_signal(
            barrier, inc=1, device_id={"branch": lax.rem(me + i, n)}, device_id_type=MESH
        )
        return c

    lax.fori_loop(1, n, greet, 0)

    count = q_ref.shape[0]
    per = heads + 2 * kvh
    some = min(count, 16)
    for r in range(0, count, some):
        for h in range(per):
            ref, g = (q_ref, h) if h < heads else (kv_ref, h - heads)
            flat[pl.ds(h, some, stride=per), :] = ref[
                r : r + some, g * HD : (g + 1) * HD
            ].astype(jnp.float32)
        for i in range(some):
            by_row[r + i] = flat[i * per : (i + 1) * per].astype(jnp.bfloat16)

    def number(j, c):
        mine = owner_ref[j]
        rank = lax.fori_loop(
            0, j, lambda i, r: r + jnp.where(owner_ref[i] == mine, 1, 0), jnp.int32(0)
        )
        slot_of[j] = mine * cap + rank
        return c

    lax.fori_loop(0, count, number, 0)

    def place(b, c):
        def scan(r, found):
            for u in range(some):
                i = r * some + u
                hit = owner_ref[i] == b
                rows_at, seen = found[:cap], found[cap]
                rows_at = [
                    jnp.where(jnp.logical_and(hit, seen == k), i, at)
                    for k, at in enumerate(rows_at)
                ]
                found = (*rows_at, seen + jnp.where(hit, 1, 0))
            return found

        found = lax.fori_loop(0, count // some, scan, (jnp.int32(0),) * (cap + 1))
        pick = pick_ref[0, b]
        length = jnp.int32(0)
        for e in range(res):
            length = jnp.where(pick == e, len_ref[e], length)
        meta_ref[b, 0:1] = jnp.full((1, HD), pick, jnp.int32)
        meta_ref[b, 1:2] = jnp.full((1, HD), length, jnp.int32)
        for k in range(cap):
            xs[b * cap + k] = by_row[found[k]]
            meta_ref[b, 2 + k : 3 + k] = jnp.full(
                (1, HD), jnp.where(found[cap] > k, 1, 0), jnp.int32
            )
        return c

    lax.fori_loop(0, n, place, 0)
    blocks = mask_ref.shape[1]
    block = pk.shape[0] // blocks
    for g in range(blocks):
        pbias[:, g * block : (g + 1) * block] = jnp.full(
            (1, block), jnp.where(mask_ref[0, g] > 0, 0.0, NEG), jnp.float32
        )
    pl.semaphore_wait(barrier, n - 1)

    def ship(src, source, e, target, way):
        return pltpu.make_async_remote_copy(
            src_ref=src,
            dst_ref=gath.at[source, e],
            send_sem=gsend.at[way, source * res + e],
            recv_sem=grecv.at[source * res + e],
            device_id={"branch": target},
            device_id_type=MESH,
        )

    def member(zz, yy, cc):
        return (zz * across + yy) * 2 + cc

    def spread(zs, e, first, act):
        source = member(zs, y, core)
        src = shared_ref.at[e] if first else gath.at[source, e]

        @pl.when(jnp.logical_and(zs <= z, z + 1 < line))
        def _():
            act(ship(src, source, e, member(lax.rem(z + 1, line), y, core), 0))

        @pl.when(jnp.logical_and(zs >= z, z >= 1))
        def _():
            act(ship(src, source, e, member(lax.rem(z + line - 1, line), y, core), 1))

        for d in range(1, across):
            act(ship(src, source, e, member(z, lax.rem(y + d, across), core), 1 + d))
        act(ship(src, source, e, sibling, 1 + across))

    def arrived(source, e):
        ship(gath.at[source, e], source, e, sibling, 0).wait_recv()

    begin = lambda copy: copy.start()
    finish = lambda copy: copy.wait_send()

    def on_line(t, act, waits):
        for up in (0, 1):
            zs = z - t if up == 0 else z + t
            ok = zs >= 0 if up == 0 else zs < line

            @pl.when(ok)
            def _():
                zc = lax.rem(zs + line, line)
                for e in range(res):
                    if waits:
                        arrived(member(zc, y, core), e)
                    spread(zc, e, False, act)

    def cross(zs, act, waits):
        for d in range(1, across):
            source = member(zs, lax.rem(y + d, across), core)
            for e in range(res):
                if waits:
                    arrived(source, e)
                act(ship(gath.at[source, e], source, e, sibling, 1 + across))

    def off_line(t, act, waits):
        @pl.when(z - t >= 0)
        def _():
            cross(lax.rem(z - t + line, line), act, waits)

        @pl.when(jnp.logical_and(z + t < line, t > 0))
        def _():
            cross(lax.rem(z + t, line), act, waits)

    def relay(t, c):
        on_line(t, begin, True)
        off_line(t - 1, begin, True)
        return c


    def part(ref, b):
        return ref.at[pl.ds(b * cap, cap)]

    def x_copy(i, b, at):
        return pltpu.make_async_remote_copy(
            src_ref=part(xs, b), dst_ref=part(xr, at), send_sem=xsend.at[i], recv_sem=xrecv.at[i],
            device_id={"branch": b}, device_id_type=MESH,
        )

    def m_copy(i, b, at):
        return pltpu.make_async_remote_copy(
            src_ref=meta_ref.at[b], dst_ref=mr.at[at], send_sem=msend.at[i], recv_sem=mrecv.at[i],
            device_id={"branch": b}, device_id_type=MESH,
        )

    def send_x(i, c):
        b = lax.rem(me + i, n)
        x_copy(i, b, me).start()
        m_copy(i, b, me).start()
        return c

    lax.fori_loop(1, n, send_x, 0)
    for e in range(res):
        spread(z, e, True, begin)
    own_x = pltpu.make_async_copy(part(xs, me), part(xr, me), lsem.at[0])
    own_m = pltpu.make_async_copy(meta_ref.at[me], mr.at[me], lsem.at[1])
    own_x.start()
    own_m.start()
    gath[me] = shared_ref[...]
    tail[...] = jnp.zeros_like(tail)

    def take_x(i, c):
        b = lax.rem(me + n - i, n)
        x_copy(i, b, b).wait_recv()
        m_copy(i, b, b).wait_recv()
        return c

    lax.fori_loop(1, n, take_x, 0)
    own_x.wait()
    own_m.wait()
    copy_k.wait()
    copy_v.wait()

    def queries(p):
        both = xr[:, pl.ds(p * 2 * GRP, 2 * GRP), :].astype(jnp.float32)
        return [
            both[:, k * GRP : (k + 1) * GRP].reshape(rows, HD).astype(jnp.bfloat16)
            for k in range(2)
        ]

    def scores(q, k):
        return lax.dot_general(q, k, (((1,), (1,)), ((), ())), preferred_element_type=jnp.float32)

    half = lax.broadcasted_iota(jnp.int32, (rows, HD), 1) < HD // 2

    def prompt_pair(p):
        for k, q in enumerate(queries(p)):
            h = 2 * p + k
            cols = slice(h * HD, (h + 1) * HD)
            s = scores(q, pk[:, cols]) * scale + pbias[...]
            m = jnp.max(s, axis=-1, keepdims=True)
            w = jnp.exp2(s - m)
            stat[h] = jnp.where(half, m, jnp.sum(w, axis=-1, keepdims=True))
            acc[h] = jnp.dot(
                w.astype(jnp.bfloat16), pv[:, cols], preferred_element_type=jnp.float32
            )

    cuts = [1 + (line - 1) * p // pairs for p in range(pairs + 1)]
    for p in range(pairs):
        prompt_pair(p)
        if cuts[p] < cuts[p + 1]:
            lax.fori_loop(cuts[p], cuts[p + 1], relay, 0)
    off_line(line - 1, begin, True)

    flat[: width * 2 * kvh] = (
        xr[:, heads:, :].astype(jnp.float32).reshape(width * 2 * kvh, HD)
    )
    for j in range(2 * kvh):
        tail[n * rlen : n * rlen + width, j * HD : (j + 1) * HD] = flat[
            pl.ds(j, width, stride=2 * kvh), :
        ].astype(jnp.bfloat16)
    col = lax.broadcasted_iota(jnp.int32, (1, tail_n), 1)

    def limits(s, carry):
        length, live = carry
        meta = mr[s]
        length = jnp.where(col // rlen == s, meta[1:2, 0:1], length)
        for k in range(cap):
            live = jnp.where(col == n * rlen + s * cap + k, meta[2 + k : 3 + k, 0:1], live)
        return length, live

    zero = jnp.zeros((1, tail_n), jnp.int32)
    length, live = lax.fori_loop(0, n, limits, (zero, zero))
    shared_ok = jnp.logical_and(col < n * rlen, lax.rem(col, rlen) < length)
    kslot[...] = jnp.where(shared_ok, -1, jnp.where(live > 0, col - n * rlen, width))
    row_slot = lax.broadcasted_iota(jnp.int32, (rows, 1), 0) // GRP

    def far(i, c):
        for yy in range(across):
            source = member(i, yy, 1 - core)
            for e in range(res):
                arrived(source, e)
        return c

    lax.fori_loop(0, line, far, 0)

    def choose(t, c):
        two = []
        for s in (2 * t, 2 * t + 1):
            pick = mr[s][0:1, 0:1]
            chosen = gath[s, 0].astype(jnp.float32)
            for e in range(1, res):
                chosen = jnp.where(pick == e, gath[s, e].astype(jnp.float32), chosen)
            two.append(chosen)
        tail[pl.ds(pl.multiple_of(t * 2 * rlen, 16), 2 * rlen), :] = jnp.concatenate(
            two, axis=0
        ).astype(jnp.bfloat16)
        return c

    lax.fori_loop(0, n // 2, choose, 0)

    def tail_pair(p):
        done = []
        for k, q in enumerate(queries(p)):
            h = 2 * p + k
            keys = tail[:, h * HD : (h + 1) * HD]
            values = tail[:, kvw + h * HD : kvw + (h + 1) * HD]
            s = jnp.where(kslot[...] <= row_slot, scores(q, keys) * scale, NEG)
            before = stat[h][:, :1]
            m = jnp.maximum(before, jnp.max(s, axis=-1, keepdims=True))
            w = jnp.exp2(s - m)
            keep = jnp.exp2(before - m)
            total = stat[h][:, HD // 2 : HD // 2 + 1] * keep + jnp.sum(w, axis=-1, keepdims=True)
            mixed = acc[h] * keep + jnp.dot(
                w.astype(jnp.bfloat16), values, preferred_element_type=jnp.float32
            )
            done.append((mixed / total).reshape(width, GRP, HD))
        ox[:, p * 2 * GRP : (p + 1) * 2 * GRP, :] = jnp.concatenate(done, axis=1).astype(
            jnp.bfloat16
        )

    def r_copy(p, i, b, at):
        cut = pl.ds(p * 2 * GRP, 2 * GRP)
        return pltpu.make_async_remote_copy(
            src_ref=ox.at[pl.ds(b * cap, cap), cut], dst_ref=orx.at[pl.ds(at * cap, cap), cut],
            send_sem=rsend.at[p, i], recv_sem=rrecv.at[p, i],
            device_id={"branch": b}, device_id_type=MESH,
        )

    def give_back(p):
        def one(i, c):
            r_copy(p, i, lax.rem(me + i, n), me).start()
            return c

        lax.fori_loop(1, n, one, 0)

    for p in range(pairs):
        tail_pair(p)
        if p:
            give_back(p - 1)
    give_back(pairs - 1)
    own_r = pltpu.make_async_copy(part(ox, me), part(orx, me), lsem.at[2])
    own_r.start()

    def sent(i, c):
        b = lax.rem(me + i, n)
        x_copy(i, b, me).wait_send()
        m_copy(i, b, me).wait_send()
        return c

    lax.fori_loop(1, n, sent, 0)
    for e in range(res):
        spread(z, e, True, finish)

    def relayed(t, c):
        on_line(t, finish, False)
        off_line(t - 1, finish, False)
        return c

    lax.fori_loop(1, line, relayed, 0)
    off_line(line - 1, finish, False)

    def returned(i, c):
        for p in range(pairs):
            r_copy(p, i, lax.rem(me + n - i, n), lax.rem(me + n - i, n)).wait_recv()
        return c

    lax.fori_loop(1, n, returned, 0)
    own_r.wait()

    for r in range(0, count, some):
        for i in range(some):
            flat[i * heads : (i + 1) * heads] = orx[slot_of[r + i]].astype(jnp.float32)
        for h in range(heads):
            out_ref[r : r + some, h * HD : (h + 1) * HD] = flat[
                pl.ds(h, some, stride=heads), :
            ].astype(jnp.bfloat16)

    def gone(i, c):
        for p in range(pairs):
            r_copy(p, i, lax.rem(me + i, n), me).wait_send()
        return c

    lax.fori_loop(1, n, gone, 0)


def body(
    across, prompt_k, prompt_v, prompt_mask, shared_kv, shared_len, send_pick,
    unique_q, unique_kv, unique_owner,
):
    n = lax.axis_size("branch")
    rows = unique_q.shape[0]
    cap = 2 * rows // n
    width = n * cap
    res, rlen = shared_kv.shape[:2]
    heads = unique_q.shape[1] // HD
    kvh = unique_kv.shape[1] // (2 * HD)
    plen = prompt_k.shape[1]
    tail_n = -(-(n * rlen + width) // 128) * 128
    qrows = width * GRP
    vmem = pl.BlockSpec(memory_space=pltpu.VMEM)
    smem = pl.BlockSpec(memory_space=pltpu.SMEM)
    anyp = pl.BlockSpec(memory_space=pl.ANY)
    bf, f32 = jnp.bfloat16, jnp.float32
    dma = pltpu.SemaphoreType.DMA
    out = pl.pallas_call(
        functools.partial(kernel, n, across, cap, rlen, res, heads),
        out_shape=jax.ShapeDtypeStruct((rows, heads * HD), bf),
        in_specs=[smem, smem, smem, smem, vmem, vmem, vmem, anyp, anyp],
        out_specs=vmem,
        scratch_shapes=[
            pltpu.VMEM(prompt_k.shape[1:], bf),
            pltpu.VMEM(prompt_v.shape[1:], bf),
            pltpu.VMEM((max(min(rows, 16) * (heads + 2 * kvh), width * 2 * kvh), HD), f32),
            pltpu.VMEM((rows, heads + 2 * kvh, HD), bf),
            pltpu.SMEM((rows,), jnp.int32),
            pltpu.VMEM((1, plen), f32),
            pltpu.VMEM((n, 2 + cap, HD), jnp.int32),
            pltpu.VMEM((width, heads + 2 * kvh, HD), bf),
            pltpu.VMEM((width, heads + 2 * kvh, HD), bf),
            pltpu.VMEM((n, 2 + cap, HD), jnp.int32),
            pltpu.VMEM((n,) + shared_kv.shape, bf),
            pltpu.VMEM((tail_n, 2 * kvh * HD), bf),
            pltpu.VMEM((1, tail_n), jnp.int32),
            pltpu.VMEM((kvh, qrows, HD), f32),
            pltpu.VMEM((kvh, qrows, HD), f32),
            pltpu.VMEM((width, heads, HD), bf),
            pltpu.VMEM((width, heads, HD), bf),
            dma((2,)),
            dma((3,)),
            dma((n,)),
            dma((n,)),
            dma((n,)),
            dma((n,)),
            dma((2 + across, n * res)),
            dma((n * res,)),
            dma((kvh // 2, n)),
            dma((kvh // 2, n)),
        ],
        compiler_params=pltpu.CompilerParams(
            collective_id=0, has_side_effects=True, vmem_limit_bytes=67043328
        ),
    )(
        unique_owner.reshape(rows), send_pick, shared_len, prompt_mask,
        unique_q, unique_kv, shared_kv, prompt_k, prompt_v,
    )
    return out


def chips_across(mesh):
    devices = mesh.devices.reshape(-1, mesh.shape["branch"])[0]
    try:
        places = [tuple(d.coords) for d in devices[::2]]
    except (AttributeError, TypeError):
        return 1
    return sum(1 for p in places if p[2] == places[0][2])


def solution(mesh):
    spec1, spec2, spec3 = (P(("groups", "branch"), *(None,) * k) for k in range(3))
    in_specs = (spec3, spec3, spec2, spec3, spec1, spec2, spec2, spec2, spec2)
    return jax.shard_map(
        functools.partial(body, chips_across(mesh)),
        mesh=mesh, in_specs=in_specs, out_specs=spec2, check_vma=False,
    )
```
